32 devices in a mesh: rep: 2 (over y), tp: 2 (over x), exp: 8 (over z, core).
Axes of the slice: x: 2, y: 2, z: 4, core: 2. Of those that a mesh axis runs over, the one named last changes fastest.
Arguments:
- attention: bfloat16 [2048, 2048], P(('rep', 'exp'), 'tp'), may hold values from -6 to 6
- stream: bfloat16 [2048, 2048], P(('rep', 'exp'), 'tp'), may hold values from -6 to 6
- proj_weight: bfloat16 [2048, 2048], P(('tp', 'exp')), may hold values from -0.125 to 0.125
- norm_gain: float32 [2048], replicated, may hold values from 0.1 to 1.9
- expert_ids: int32 [2048, 8], P(('rep', 'exp')), may hold values from 0 to 31, all different within a row; in each aligned block of 128 rows (0 to 127, 128 to 255, ...) at most 40 rows name the same one
- gate_fixed: int32 [2048, 8], P(('rep', 'exp')), may hold values from 1 to 65535
- w_gate: bfloat16 [32, 2048, 512], P('exp', None, 'tp'), may hold values from -0.125 to 0.125
- w_up: bfloat16 [32, 2048, 512], P('exp', None, 'tp'), may hold values from -0.125 to 0.125
- w_down: bfloat16 [32, 512, 2048], P('exp', 'tp'), may hold values from -0.25 to 0.25
- gradient: float32 [2, 2048, 2048], P('rep', ('tp', 'exp')), may hold values from -6 to 6
- feedback: float32 [2, 2048, 2048], P('rep', ('tp', 'exp')), may hold values from -4 to 4
- block_ids: int32 [2, 16, 64], P('rep', ('tp', 'exp')), may hold values from 0 to 2047, as said below
Outputs:
- output: bfloat16 [2048, 2048], P(('rep', 'exp'), 'tp')
- update: float32 [2048, 2048], P(('tp', 'exp'))
- new_error: float32 [2, 2048, 2048], P('rep', ('tp', 'exp'))
The draws below stay inside these ranges and needn't reach their ends.
Inputs may be any that keep to these rules, and one draw needn't show every extreme that they name: `expert_ids`: each row names 8 different experts; within each aligned block of 128 rows no expert is named by more than 40 rows, a bound that some block reaches. `block_ids`: the 64 block numbers of one replica's row group are distinct.
All inputs are finite; a program needn't handle non-finite values.
Results may differ from the reference program's by a relative error of at most 0.0064.
Values may be sent and summed in bfloat16 or wider, within the bound.
No kernel may reach another device: no remote copies, remote signals or barrier semaphores. Data moves between devices by JAX's collectives and lax.ppermute only.
A program may use at most 64 MiB of HBM per device.

```python
import math
import jax
import jax.numpy as jnp
import numpy as np
from jax import lax

D = 2048
A = 2048
FF = 512
EXPERTS = 32
TOP = 8
TOK_DEV = 128
BLK = 128
KB = 64
FF_DEV = 256
CAP = 40
TOKENS = 2048
REPLICAS = 2
SHARDS = 16
NBLK = 2048
N_TP = 2


def draw_block_ids(key, part):
    scores = jax.random.randint(key, (REPLICAS, SHARDS, NBLK), 0, 1 << 20, dtype=jnp.int32)
    scores = scores * NBLK + jnp.arange(NBLK, dtype=jnp.int32)
    scores = scores.at[0, 0, NBLK - 1].set(-2).at[0, 0, 0].set(-1)
    order = jnp.argsort(scores, axis=-1)
    return order[..., :KB].astype(jnp.int32)


def place_ends(result, own_key, least, largest):
    extent = result.shape
    index_at = [jax.random.randint(jax.random.fold_in(own_key, axis), (), 0, extent[axis]) for axis in range(len(extent))]
    result = result.at[tuple(index_at)].set(least)
    longest = extent.index(max(extent))
    index_at[longest] = (index_at[longest] + 1) % extent[longest]
    return result.at[tuple(index_at)].set(largest)


def level_of(key, shape, split, smallest, high):
    loudness, own = 1.0, jax.random.fold_in(key, 6)
    for position, shards_of in split:
        heights = jnp.exp(jax.random.uniform(jax.random.fold_in(own, position), (shards_of,), jnp.float32, smallest / len(split), high / len(split)))
        loudness = loudness * jnp.repeat(heights, shape[position] // shards_of).reshape([-1 if axis == position else 1 for axis in range(len(shape))])
    return loudness


def shared_out(rng, own, number, rows, count, top, most, slope):
    sequence = jax.random.permutation(rng, count)
    heavy_load, common = load_shares(count, rows * top, most, slope, True), load_shares(count, rows * top, most, slope, False)
    places = jnp.arange(count)

    def named(tallies, turn):
        used = int((tallies > 0).sum())
        fixed = max(1, used // 4)
        moved = fixed + (places - fixed + turn * (used - fixed)) % max(1, count - fixed)
        return jnp.zeros((count,), jnp.int32).at[sequence[jnp.where(places < fixed, places, moved)]].set(jnp.asarray(tallies, jnp.int32))

    tallies = jnp.where(number % 4 == 0, named(heavy_load, number // 4), named(common, number - number // 4 - 1))
    mixed = jax.random.permutation(jax.random.fold_in(own, 3), count)
    giver, taker = mixed[0:count // 2 * 2:2], mixed[1:count // 2 * 2:2]
    margin = jnp.minimum(tallies[giver] - 1, most - tallies[taker]) // 2
    margin = jnp.where((giver == sequence[0]) | (taker == sequence[0]) | (tallies[taker] == 0), 0, jnp.maximum(margin, 0))
    moved = jax.random.randint(jax.random.fold_in(own, 4), (count // 2,), 0, 1 << 20) % (margin + 1)
    tallies = tallies.at[giver].add(-moved).at[taker].add(moved)
    labels = jnp.searchsorted(jnp.cumsum(tallies), jnp.arange(rows * top), side="right").astype(jnp.int32)
    table = labels.reshape(top, rows).T
    table = table[jax.random.permutation(jax.random.fold_in(own, 1), rows)]
    turn = jax.random.randint(jax.random.fold_in(own, 2), (rows, 1), 0, top)
    return jnp.take_along_axis(table, (jnp.arange(top)[None, :] + turn) % top, axis=1)


def load_shares(amount, total, most, lean, full):
    weights = [(1 << 20) // math.isqrt(standing ** lean) + 1 for standing in range(1, amount + 1)]
    largest = most if full else min(most, max(-(-total // amount), total * weights[0] // sum(weights)))
    least = 1 if total - largest >= amount - 1 else 0
    given, surplus = [largest] + [least] * (amount - 1), total - largest - least * (amount - 1)
    while surplus > 0:
        candidates = [i for i in range(1, amount) if given[i] < largest] or [i for i in range(1, amount) if given[i] < most]
        pool, left = sum([weights[i] for i in candidates]), surplus
        for i in candidates:
            extra = min(most - given[i], max(1, left * weights[i] // pool), surplus)
            given[i] = given[i] + extra
            surplus = surplus - extra
    return np.array(given)


def centred(own_key, dims, deviation, reach, split=(), kind=jnp.bfloat16):
    entries = deviation * jax.random.normal(own_key, dims, jnp.float32)
    if split:
        entries = entries * level_of(own_key, dims, split, -0.22, 0.18)
    return jnp.clip(entries, -reach, reach).astype(kind)


def setup_inputs(seed: int = 0) -> dict:
    arg_keys = jax.random.split(jax.random.key(seed), 13)
    attention = centred(arg_keys[0], (TOKENS, A), 1.0, 6.0, ((0, 16), (1, 2)))
    stream = centred(arg_keys[1], (TOKENS, D), 1.0, 6.0, ((0, 16), (1, 2)))
    proj_weight = centred(arg_keys[2], (A, D), A ** -0.5, 0.125, ((0, 16),))
    norm_gain = jnp.clip(1.0 + 0.18 * jax.random.normal(arg_keys[3], (D,), jnp.float32), 0.1, 1.9)
    expert_ids_keys = jax.random.split(jax.random.fold_in(arg_keys[4], 1), TOKENS // TOK_DEV)
    expert_ids_turns = jax.random.permutation(jax.random.fold_in(arg_keys[4], 3), TOKENS // TOK_DEV)
    expert_ids = jax.vmap(lambda own, number: shared_out(jax.random.fold_in(arg_keys[4], 2), own, number, TOK_DEV, EXPERTS, TOP, CAP, 2))(expert_ids_keys, expert_ids_turns).reshape((TOKENS, TOP))
    gate_fixed = place_ends(jax.random.randint(arg_keys[5], (TOKENS, TOP), 1, 65536), jax.random.fold_in(arg_keys[5], 1), 1, 65535).astype(jnp.int32)
    w_gate = centred(arg_keys[6], (EXPERTS, D, FF), D ** -0.5, 0.125, ((0, 8), (2, 2)))
    w_up = centred(arg_keys[7], (EXPERTS, D, FF), D ** -0.5, 0.125, ((0, 8), (2, 2)))
    w_down = centred(arg_keys[8], (EXPERTS, FF, D), FF ** -0.5, 0.25, ((0, 8), (1, 2)))
    gradient = centred(arg_keys[9], (REPLICAS, A, D), 1.0, 6.0, ((0, 2), (1, 16)), jnp.float32)
    feedback = centred(arg_keys[10], (REPLICAS, A, D), 0.5, 4.0, ((0, 2), (1, 16)), jnp.float32)
    block_ids = draw_block_ids(jax.random.fold_in(arg_keys[12], 71), 0)
    return dict(attention=attention, stream=stream, proj_weight=proj_weight, norm_gain=norm_gain, expert_ids=expert_ids, gate_fixed=gate_fixed, w_gate=w_gate, w_up=w_up, w_down=w_down, gradient=gradient, feedback=feedback, block_ids=block_ids)


def slot_position(ids_block):
    flat_ids = ids_block.reshape(-1)
    table = (flat_ids[:, None] == jnp.arange(EXPERTS, dtype=jnp.int32)[None, :]).astype(jnp.int32)
    before = jnp.cumsum(table, axis=0) - table
    return lax.optimization_barrier(jnp.sum(before * table, axis=1)).astype(jnp.int32)

def reference(attention, stream, proj_weight, norm_gain, expert_ids, gate_fixed, w_gate, w_up, w_down, gradient, feedback, block_ids):
    residual = (stream.astype(jnp.float32) + jnp.dot(attention, proj_weight, preferred_element_type=jnp.float32)).astype(jnp.bfloat16)
    res_float = residual.astype(jnp.float32)
    scale = lax.rsqrt(lax.optimization_barrier(jnp.mean(res_float * res_float, axis=1, keepdims=True)) + 1e-06)
    normed = (res_float * scale * norm_gain).astype(jnp.bfloat16)
    num_blocks = TOKENS // TOK_DEV
    positions = jax.vmap(slot_position)(expert_ids.reshape(num_blocks, TOK_DEV, TOP)).reshape(-1)
    flat_ids = expert_ids.reshape(-1)
    token_of = (jnp.arange(TOKENS * TOP, dtype=jnp.int32) // TOP).astype(jnp.int32)
    block_of = (token_of // TOK_DEV).astype(jnp.int32)
    slot = (block_of * CAP + positions).astype(jnp.int32)
    gate_flat = gate_fixed.reshape(-1).astype(jnp.float32) / 65536.0
    buffer_rows = num_blocks * CAP

    def one_expert(expert, total):
        target = jnp.where(flat_ids == expert, slot, buffer_rows).astype(jnp.int32)
        holder = jnp.full((buffer_rows,), TOKENS, jnp.int32).at[target].set(token_of, mode='drop')
        weight = jnp.zeros((buffer_rows,), jnp.float32).at[target].set(gate_flat, mode='drop')
        rows_in = jnp.take(normed, holder, axis=0, mode='fill', fill_value=0)
        gate = jnp.dot(rows_in, w_gate[expert], preferred_element_type=jnp.float32)
        upper = jnp.dot(rows_in, w_up[expert], preferred_element_type=jnp.float32)
        hidden = (jax.nn.silu(gate) * upper).astype(jnp.bfloat16)
        groups = hidden.reshape(buffer_rows, N_TP, FF_DEV).astype(jnp.float32)
        down = w_down[expert].reshape(N_TP, FF_DEV, D).astype(jnp.float32)
        parts = jnp.einsum('rgf,gfd->rgd', groups, down, precision=lax.Precision.HIGHEST).astype(jnp.bfloat16)
        parts = lax.optimization_barrier(parts).astype(jnp.float32)
        combined = lax.optimization_barrier(jnp.sum(parts, axis=1)).astype(jnp.bfloat16)
        combined = lax.optimization_barrier(combined).astype(jnp.float32)
        return total.at[holder].add(combined * weight[:, None], mode='drop')
    mixed = lax.fori_loop(0, EXPERTS, one_expert, jnp.zeros((TOKENS, D), jnp.float32))
    output = (res_float + mixed).astype(jnp.bfloat16)
    accumulated = gradient + feedback
    blocks = accumulated.reshape(REPLICAS, SHARDS, NBLK, BLK)
    chosen = jnp.any(block_ids[:, :, :, None] == jnp.arange(NBLK, dtype=jnp.int32)[None, None, None, :], axis=2)
    mask = chosen.astype(jnp.float32)[..., None]
    update = (lax.optimization_barrier(jnp.sum(blocks * mask, axis=0)) / REPLICAS).reshape(A, D)
    new_error = (blocks * (1.0 - mask)).reshape(REPLICAS, A, D)
    return (output, update, new_error)
```

```python
import functools

import jax
import jax.numpy as jnp
from jax import lax
from jax.experimental import pallas as pl
from jax.experimental.pallas import tpu as pltpu
from jax.sharding import PartitionSpec as P

EXPERTS = 32
BLK = 128
CORES = 2

F32 = jnp.float32
BF16 = jnp.bfloat16
VMEM = pl.BlockSpec(memory_space=pltpu.VMEM)
SMEM = pl.BlockSpec(memory_space=pltpu.SMEM)


def project_kernel(senders, where_ref, own_ref, far_ref, own_core_ref, far_core_ref, side_ref, side_core_ref, *rest):
    weights, (mine_ref, peer_ref, full_ref) = rest[:senders], rest[senders:]
    rows = weights[0].shape[2]
    core = where_ref[2]
    for turn in range(senders):
        at = where_ref[3 + turn]
        for part in range(2):
            for rel in range(2):
                which = core if rel == 0 else 1 - core
                start = pl.multiple_of((at * CORES + which) * rows, rows)
                full_ref[part, pl.ds(start, rows), :] = weights[turn][part, rel]
    for rel, (near, far, side) in enumerate(
        ((own_ref, far_ref, side_ref), (own_core_ref, far_core_ref, side_core_ref))
    ):
        groups, tok, depth = near.shape
        total = jnp.dot(near[...].reshape(groups * tok, depth), full_ref[0], preferred_element_type=F32)
        total += jnp.dot(far[...].reshape(groups * tok, depth), full_ref[1], preferred_element_type=F32)
        for group, out_ref in enumerate((mine_ref, peer_ref)):
            piece = total[group * tok : (group + 1) * tok] + side[group].astype(F32)
            out_ref[rel] = piece.astype(BF16)


def expert_kernel(
    where_ref, a_ref, b_ref, ac_ref, bc_ref, mix_ref, gain_ref, gate_ref, up_ref, down_ref, keep_ref, send_ref, x_ref, h_ref
):
    x, y, core, home = where_ref[0], where_ref[1], where_ref[2], where_ref[3]
    tok = a_ref.shape[2]
    piece = a_ref.shape[3]
    width = x_ref.shape[1]
    local, ff = gate_ref.shape[0], gate_ref.shape[2]

    def offset(xrel, yrel, crel):
        xx = x if xrel == 0 else 1 - x
        yy = y if yrel == 0 else 1 - y
        cc = core if crel == 0 else 1 - core
        return pl.multiple_of(((xx * 2 + yy) * CORES + cc) * piece, piece)

    for rel in range(2):
        pieces = []
        for xrel, crel, ref in ((0, 0, a_ref), (1, 0, b_ref), (0, 1, ac_ref), (1, 1, bc_ref)):
            for yrel in range(2):
                at = rel if crel == 0 else 1 - rel
                pieces.append((offset(xrel, yrel, crel), ref[yrel, at].astype(F32)))
        square = pieces[0][1] * pieces[0][1]
        for _, value in pieces[1:]:
            square += value * value
        scale = lax.rsqrt(jnp.sum(square, axis=1, keepdims=True) / width + 1e-06)
        for start, value in pieces:
            gain = gain_ref[:, pl.ds(start, piece)]
            x_ref[rel * tok : (rel + 1) * tok, pl.ds(start, piece)] = (value * scale * gain).astype(BF16)
    rows = x_ref[...]
    first = pl.multiple_of((home * CORES + core) * tok, tok)
    second = pl.multiple_of((home * CORES + 1 - core) * tok, tok)
    mix = jnp.concatenate([mix_ref[pl.ds(first, tok), :], mix_ref[pl.ds(second, tok), :]], axis=0)
    for j in range(local):
        gate = jnp.dot(rows, gate_ref[j], preferred_element_type=F32)
        upper = jnp.dot(rows, up_ref[j], preferred_element_type=F32)
        hidden = gate / (1.0 + jnp.exp(-gate)) * upper
        h_ref[:, j * ff : (j + 1) * ff] = (hidden * mix[:, j : j + 1]).astype(BF16)
    inner = h_ref[...]
    half = width // 2
    step = half // 2
    for xrel in range(2):
        xx = x if xrel == 0 else 1 - x
        for part in range(2):
            start = pl.multiple_of(xx * half + part * step, step)
            made = jnp.dot(inner, down_ref[:, pl.ds(start, step)], preferred_element_type=F32)
            keep_ref[xrel, :, part * step : (part + 1) * step] = made[:tok]
            send_ref[xrel, :, part * step : (part + 1) * step] = made[tok:].astype(BF16)


def finish_kernel(count, where_ref, a_ref, ac_ref, *rest):
    parts, out_ref = rest[:count], rest[count]
    y, core = where_ref[1], where_ref[2]
    piece = a_ref.shape[3]
    for yrel in range(2):
        yy = y if yrel == 0 else 1 - y
        for crel, ref in ((0, a_ref), (1, ac_ref)):
            cc = core if crel == 0 else 1 - core
            start = pl.multiple_of((yy * CORES + cc) * piece, piece)
            total = ref[yrel, crel].astype(F32)
            for part in parts:
                total += part[:, pl.ds(start, piece)].astype(F32)
            out_ref[:, pl.ds(start, piece)] = total.astype(BF16)


def cut(value, start, size):
    return lax.dynamic_slice_in_dim(value, start, size, value.ndim - 1)


def turns(count):
    order, low, high = [], 1, count - 1
    while low <= high:
        order.append(low)
        if high != low:
            order.append(high)
        low, high = low + 1, high - 1
    return order


def on_device(
    attention,
    stream,
    proj_weight,
    norm_gain,
    expert_ids,
    gate_fixed,
    w_gate,
    w_up,
    w_down,
    gradient,
    feedback,
    block_ids,
):
    replicas, members = lax.axis_size("rep"), lax.axis_size("exp")
    stack = members // CORES
    x, r, e = lax.axis_index("tp"), lax.axis_index("rep"), lax.axis_index("exp")
    y, z, core = r % 2, e // CORES, e % CORES
    tok, half = stream.shape
    width = half * 2
    quarter, piece = half // 2, half // 4
    local, ff = w_gate.shape[0], w_gate.shape[2]

    over_x = functools.partial(lax.ppermute, axis_name="tp", perm=[(0, 1), (1, 0)])
    over_y = functools.partial(lax.ppermute, axis_name="rep", perm=[(i, i ^ 1) for i in range(replicas)])
    over_core = functools.partial(lax.ppermute, axis_name="exp", perm=[(i, i ^ 1) for i in range(members)])

    def over_z(value, by):
        perm = [(i, (i + by * CORES) % members) for i in range(members)]
        return lax.ppermute(value, "exp", perm)

    place = jnp.stack([x, y, core])
    order = turns(stack)
    homes = [z] + [(z - by) % stack for by in order]

    weight_far = over_x(cut(proj_weight, (1 - x) * half + y * quarter, quarter))
    weight_two = jnp.stack([cut(proj_weight, x * half + y * quarter, quarter), weight_far])
    weight_core = over_core(cut(weight_two, (1 - core) * piece, piece))
    weight_block = jnp.stack([cut(weight_two, core * piece, piece), weight_core], axis=1)
    blocks = [weight_block] + [over_z(weight_block, by) for by in order]

    sent = jnp.concatenate([attention, cut(stream, (1 - y) * quarter, quarter)], axis=1)
    came = over_y(sent)
    near = jnp.stack([attention, came[:, :half]])
    side = jnp.stack([cut(stream, y * quarter, quarter), came[:, half:]])
    far = over_x(near)
    near_core, far_core = over_core(near), over_core(far)
    side_core = over_core(cut(side, (1 - core) * piece, piece))
    side = cut(side, core * piece, piece)

    ids, fixed = expert_ids.T, gate_fixed.T.astype(F32) / 65536.0
    named = ids[:, None, :] == jnp.arange(EXPERTS, dtype=jnp.int32)[None, :, None]
    table = jnp.sum(jnp.where(named, fixed[:, None, :], 0.0), axis=0)
    table = lax.all_to_all(table, "exp", split_axis=0, concat_axis=0, tiled=True)
    mix = table.reshape(members, local, tok).transpose(0, 2, 1).reshape(members * tok, local)

    slab = jax.ShapeDtypeStruct((2, tok, piece), BF16)
    mine, peer = pl.pallas_call(
        functools.partial(project_kernel, stack),
        in_specs=[SMEM] + [VMEM] * (6 + stack),
        out_specs=(VMEM, VMEM),
        out_shape=(slab, slab),
        scratch_shapes=[pltpu.VMEM((2, half, piece), BF16)],
        name="project",
    )(jnp.concatenate([place, jnp.stack(homes)]), near, far, near_core, far_core, side, side_core, *blocks)
    rows = jnp.stack([mine, over_y(peer)])

    gain = norm_gain.reshape(1, width)
    down = w_down.reshape(local * ff, width)

    def run(home, a):
        b = over_x(a)
        ac, bc = over_core(a), over_core(b)
        keep, send = pl.pallas_call(
            expert_kernel,
            in_specs=[SMEM] + [VMEM] * 9,
            out_specs=(VMEM, VMEM),
            out_shape=(
                jax.ShapeDtypeStruct((2, tok, half), F32),
                jax.ShapeDtypeStruct((2, tok, half), BF16),
            ),
            scratch_shapes=[pltpu.VMEM((2 * tok, width), BF16), pltpu.VMEM((2 * tok, local * ff), BF16)],
            name="experts",
        )(jnp.concatenate([place, home[None]]), a, b, ac, bc, mix, gain, w_gate, w_up, down)
        other = over_core(send).astype(F32)
        beyond = over_x((keep[1] + other[1]).astype(BF16)).astype(F32)
        return keep[0] + other[0] + beyond, ac

    arrived = [over_z(rows, by) for by in order]
    total, rows_core = run(z, rows)
    parts = [total]
    for by, home, block in zip(order, homes[1:], arrived):
        made, _ = run(home, block)
        parts.append(over_z(made.astype(BF16), -by))
    output = pl.pallas_call(
        functools.partial(finish_kernel, len(parts)),
        in_specs=[SMEM] + [VMEM] * (2 + len(parts)),
        out_specs=VMEM,
        out_shape=jax.ShapeDtypeStruct((tok, half), BF16),
        name="finish",
    )(place, rows, rows_core, *parts)

    accumulated = (gradient + feedback)[0]
    height, depth = accumulated.shape
    across = depth // BLK
    chosen = block_ids.reshape(-1)
    row_hit = (jnp.arange(height, dtype=jnp.int32)[:, None] == chosen[None, :] // across).astype(BF16)
    col_hit = (jnp.arange(depth, dtype=jnp.int32)[None, :] // BLK == chosen[:, None] % across).astype(BF16)
    hit = jnp.dot(row_hit, col_hit, preferred_element_type=F32) > 0.5
    picked = jnp.where(hit, accumulated, 0.0)
    remaining = jnp.where(hit, 0.0, accumulated)[None]
    moved = picked.astype(BF16)
    update = picked
    for by in range(1, replicas):
        perm = [(i, (i + by) % replicas) for i in range(replicas)]
        update = update + lax.ppermute(moved, "rep", perm).astype(F32)
    return (output, update / replicas, remaining)


def solution(mesh):
    in_specs = (
        P(("rep", "exp"), "tp"),
        P(("rep", "exp"), "tp"),
        P(("tp", "exp"), None),
        P(),
        P(("rep", "exp"), None),
        P(("rep", "exp"), None),
        P("exp", None, "tp"),
        P("exp", None, "tp"),
        P("exp", "tp", None),
        P("rep", ("tp", "exp"), None),
        P("rep", ("tp", "exp"), None),
        P("rep", ("tp", "exp"), None),
    )
    out_specs = (P(("rep", "exp"), "tp"), P(("tp", "exp"), None), P("rep", ("tp", "exp"), None))
    return jax.shard_map(
        on_device, mesh=mesh, in_specs=in_specs, out_specs=out_specs, check_vma=False
    )
```

```python
import functools

import jax
import jax.numpy as jnp
from jax import lax
from jax.experimental import pallas as pl
from jax.experimental.pallas import tpu as pltpu
from jax.sharding import PartitionSpec as P


EXPERTS = 32
BLK = 128
CORES = 2

F32 = jnp.float32
BF16 = jnp.bfloat16
VMEM = pl.BlockSpec(memory_space=pltpu.VMEM)
SMEM = pl.BlockSpec(memory_space=pltpu.SMEM)


def project_kernel(turn, where_ref, *rest):
    own_ref, far0_ref, far1_ref, own_core_ref, far0_core_ref, far1_core_ref, side_ref, side_core_ref, *rest = rest
    weights, (mine_ref, peer_ref, full_ref) = rest[: len(turn)], rest[len(turn) :]
    rows = weights[0].shape[2]
    core = where_ref[2]
    for by, block_ref in zip(turn, weights):
        at = where_ref[3] ^ by
        for part in range(2):
            for rel in range(2):
                which = core if rel == 0 else 1 - core
                start = pl.multiple_of((at * CORES + which) * rows, rows)
                full_ref[part, pl.ds(start, rows), :] = block_ref[part, rel]
    for rel, (near, fars, side) in enumerate(
        (
            (own_ref, (far0_ref, far1_ref), side_ref),
            (own_core_ref, (far0_core_ref, far1_core_ref), side_core_ref),
        )
    ):
        for group, (far, out_ref) in enumerate(zip(fars, (mine_ref, peer_ref))):
            total = jnp.dot(near[group], full_ref[0], preferred_element_type=F32)
            total += jnp.dot(far[...], full_ref[1], preferred_element_type=F32)
            out_ref[rel] = (total + side[group].astype(F32)).astype(BF16)


def hold_kernel(*refs):
    sources, targets, sem = refs[:3], refs[3:6], refs[6]
    copies = [pltpu.make_async_copy(a, b, sem.at[i]) for i, (a, b) in enumerate(zip(sources, targets))]
    for copy in copies:
        copy.start()
    for copy in copies:
        copy.wait()


def column(row):
    size = row.shape[1]
    same = lax.broadcasted_iota(jnp.int32, (size, size), 0) == lax.broadcasted_iota(jnp.int32, (size, size), 1)
    return jnp.sum(jnp.where(same, jnp.broadcast_to(row, (size, size)), 0.0), axis=1, keepdims=True)


def expert_kernel(
    where_ref, a_ref, b_ref, ac_ref, bc_ref, mix_ref, gain_ref, gate_ref, up_ref, down_ref, keep_ref, send_ref, x_ref, h_ref
):
    x, y, core, z = where_ref[0], where_ref[1], where_ref[2], where_ref[3]
    tok = a_ref.shape[2]
    piece = a_ref.shape[3]
    width = x_ref.shape[1]
    local, ff = gate_ref.shape[0], gate_ref.shape[2]

    def offset(xrel, yrel, crel):
        xx = x if xrel == 0 else 1 - x
        yy = y if yrel == 0 else 1 - y
        cc = core if crel == 0 else 1 - core
        return pl.multiple_of(((xx * 2 + yy) * CORES + cc) * piece, piece)

    for rel in range(2):
        pieces = []
        for xrel, crel, ref in ((0, 0, a_ref), (1, 0, b_ref), (0, 1, ac_ref), (1, 1, bc_ref)):
            for yrel in range(2):
                at = rel if crel == 0 else 1 - rel
                pieces.append((offset(xrel, yrel, crel), ref[yrel, at].astype(F32)))
        square = pieces[0][1] * pieces[0][1]
        for _, value in pieces[1:]:
            square += value * value
        scale = lax.rsqrt(jnp.sum(square, axis=1, keepdims=True) / width + 1e-06)
        for start, value in pieces:
            gain = gain_ref[:, pl.ds(start, piece)]
            x_ref[rel * tok : (rel + 1) * tok, pl.ds(start, piece)] = (value * scale * gain).astype(BF16)
    rows = x_ref[...]
    own = (z * CORES + core) * local
    for j in range(local):
        gate = jnp.dot(rows, gate_ref[j], preferred_element_type=F32)
        upper = jnp.dot(rows, up_ref[j], preferred_element_type=F32)
        hidden = gate / (1.0 + jnp.exp(-gate)) * upper
        mix = jnp.concatenate([column(mix_ref[rel, pl.ds(own + j, 1), :]) for rel in range(2)], axis=0)
        h_ref[:, j * ff : (j + 1) * ff] = (hidden * mix).astype(BF16)
    inner = h_ref[...]
    half = width // 2
    step = half // 2
    for xrel in range(2):
        xx = x if xrel == 0 else 1 - x
        for part in range(2):
            start = pl.multiple_of(xx * half + part * step, step)
            made = jnp.dot(inner, down_ref[:, pl.ds(start, step)], preferred_element_type=F32)
            keep_ref[xrel, :, part * step : (part + 1) * step] = made[:tok]
            send_ref[xrel, :, part * step : (part + 1) * step] = made[tok:].astype(BF16)


def finish_kernel(count, where_ref, a_ref, ac_ref, *rest):
    parts, out_ref = rest[:count], rest[count]
    y, core = where_ref[1], where_ref[2]
    piece = a_ref.shape[3]
    for yrel in range(2):
        yy = y if yrel == 0 else 1 - y
        for crel, ref in ((0, a_ref), (1, ac_ref)):
            cc = core if crel == 0 else 1 - core
            start = pl.multiple_of((yy * CORES + cc) * piece, piece)
            total = ref[yrel, crel].astype(F32)
            for part in parts:
                total += part[:, pl.ds(start, piece)].astype(F32)
            out_ref[:, pl.ds(start, piece)] = total.astype(BF16)


def pick_kernel(row_ref, col_ref, gradient_ref, feedback_ref, rest_ref, picked_ref, moved_ref):
    height, depth = gradient_ref.shape
    count = row_ref.shape[1]
    row_hit = (lax.broadcasted_iota(jnp.int32, (height, count), 0) == row_ref[...]).astype(F32).astype(BF16)
    place = lax.broadcasted_iota(jnp.int32, (depth, count), 0) - col_ref[...] * BLK
    col_hit = ((place >= 0) & (place < BLK)).astype(F32).astype(BF16)
    hit = lax.dot_general(row_hit, col_hit, (((1,), (1,)), ((), ())), preferred_element_type=F32) > 0.5
    value = gradient_ref[...] + feedback_ref[...]
    picked = jnp.where(hit, value, 0.0)
    rest_ref[...] = jnp.where(hit, 0.0, value)
    picked_ref[...] = picked
    moved_ref[...] = picked.astype(BF16)


def cut(value, start, size):
    return lax.dynamic_slice_in_dim(value, start, size, value.ndim - 1)


def turns(count):
    return list(range(1, count))


def layer(
    attention,
    stream,
    proj_weight,
    norm_gain,
    expert_ids,
    gate_fixed,
    w_gate,
    w_up,
    w_down,
    gradient,
    feedback,
    block_ids,
):
    replicas, members = lax.axis_size("rep"), lax.axis_size("exp")
    stack = members // CORES
    x, r, e = (lax.axis_index(axis).astype(jnp.uint32) for axis in ("tp", "rep", "exp"))
    two, cores = jnp.uint32(2), jnp.uint32(CORES)
    y, z, core = lax.rem(r, two), lax.div(e, cores), lax.rem(e, cores)
    tok, half = stream.shape
    width = half * 2
    quarter, piece = half // 2, half // 4
    local, ff = w_gate.shape[0], w_gate.shape[2]

    order = turns(stack)

    swap = [(0, 1), (1, 0)]
    pair = [(i, i ^ 1) for i in range(members)]
    cross = [(i * members + j, (1 - i) * members + (j ^ 1)) for i in range(2) for j in range(members)]

    def over_x(value):
        return lax.ppermute(value, "tp", swap)

    def over_core(value):
        return lax.ppermute(value, "exp", pair)

    def over_both(value):
        return lax.ppermute(value, ("tp", "exp"), cross)

    def over_y(value):
        return lax.ppermute(value, "rep", [(i, i ^ 1) for i in range(replicas)])

    def over_z(value, by):
        return lax.ppermute(value, "exp", [(i, i ^ (by * CORES)) for i in range(members)])

    def spread(value):
        held = {0: value}
        for by in order:
            low = by & -by
            held[by] = over_z(held[by ^ low], low)
        return [held[by] for by in [0] + order]

    place = jnp.stack([x, y, core, z]).astype(jnp.int32)
    place, proj_weight = lax.optimization_barrier((place, proj_weight))

    near_cols, far_cols = x * half + y * quarter, (1 - x) * half + y * quarter
    weight_far = over_x(cut(proj_weight, far_cols + core * piece, piece))
    weight_both = over_both(cut(proj_weight, far_cols + (1 - core) * piece, piece))
    weight_core = over_core(cut(proj_weight, near_cols + (1 - core) * piece, piece))
    weight_own = cut(proj_weight, near_cols + core * piece, piece)
    weight_block = jnp.stack([weight_own, weight_core, weight_far, weight_both])
    weight_block = weight_block.reshape(2, 2, *weight_own.shape)
    blocks = spread(weight_block)

    sent = jnp.concatenate([attention, cut(stream, (1 - y) * quarter, quarter)], axis=1)
    far_mine = over_x(attention)
    came = over_y(sent)
    near = jnp.stack([attention, came[:, :half]])
    side = jnp.stack([cut(stream, y * quarter, quarter), came[:, half:]])
    far_peer = over_x(near[1])
    near_core = over_core(near)
    far = (far_mine, far_peer)
    side_core = over_core(cut(side, (1 - core) * piece, piece))
    side = cut(side, core * piece, piece)

    ids, fixed = expert_ids.T, gate_fixed.T.astype(F32) / 65536.0
    named = ids[:, None, :] == jnp.arange(EXPERTS, dtype=jnp.int32)[None, :, None]
    table = jnp.sum(jnp.where(named, fixed[:, None, :], 0.0), axis=0)
    table = jnp.stack([table, over_core(table)])
    mixes, bit = {0: table}, stack // 2
    while bit:
        known = list(mixes)
        moved = over_z(jnp.stack([mixes[by] for by in known]), bit)
        mixes.update({by ^ bit: moved[i] for i, by in enumerate(known)})
        bit //= 2

    far_core = (over_core(far_mine), over_core(far_peer))
    slab = jax.ShapeDtypeStruct((2, tok, piece), BF16)
    mine, peer = pl.pallas_call(
        functools.partial(project_kernel, [0] + order),
        in_specs=[SMEM] + [VMEM] * (8 + stack),
        out_specs=(VMEM, VMEM),
        out_shape=(slab, slab),
        scratch_shapes=[pltpu.VMEM((2, half, piece), BF16)],
        name="project",
        compiler_params=pltpu.CompilerParams(vmem_limit_bytes=4 << 20),
    )(place, near, *far, near_core, *far_core, side, side_core, *blocks)
    rows = jnp.stack([mine, over_y(peer)])

    gain = norm_gain.reshape(1, width)
    source = (w_gate, w_up, w_down.reshape(local * ff, width))
    hold = pl.pallas_call(
        hold_kernel,
        in_specs=[pl.BlockSpec(memory_space=pl.ANY)] * 3,
        out_specs=(VMEM,) * 3,
        out_shape=tuple(jax.ShapeDtypeStruct(w.shape, w.dtype) for w in source),
        scratch_shapes=[pltpu.SemaphoreType.DMA((3,))],
        name="hold",
        compiler_params=pltpu.CompilerParams(vmem_limit_bytes=36 << 20),
    )
    held = hold(*source)

    def run(a, mix):
        b = over_x(a)
        ac, bc = over_core(a), over_core(b)
        call = pl.pallas_call(
            expert_kernel,
            in_specs=[SMEM] + [VMEM] * 9,
            out_specs=(VMEM, VMEM),
            out_shape=(
                jax.ShapeDtypeStruct((2, tok, half), F32),
                jax.ShapeDtypeStruct((2, tok, half), BF16),
            ),
            scratch_shapes=[pltpu.VMEM((2 * tok, width), BF16), pltpu.VMEM((2 * tok, local * ff), BF16)],
            name="experts",
            compiler_params=pltpu.CompilerParams(vmem_limit_bytes=6 << 20),
        )
        keep, give = call(place, a, b, ac, bc, mix, gain, *held)
        other = over_core(give).astype(F32)
        beyond = over_x((keep[1] + other[1]).astype(BF16)).astype(F32)
        return keep[0] + other[0] + beyond, ac

    arrived = spread(rows)[1:]
    total, rows_core = run(rows, mixes[0])
    parts = [total]
    for by, block in zip(order, arrived):
        made, _ = run(block, mixes[by])
        parts.append(over_z(made.astype(BF16), by))
    output = pl.pallas_call(
        functools.partial(finish_kernel, len(parts)),
        in_specs=[SMEM] + [VMEM] * (2 + len(parts)),
        out_specs=VMEM,
        out_shape=jax.ShapeDtypeStruct((tok, half), BF16),
        name="finish",
        compiler_params=pltpu.CompilerParams(vmem_limit_bytes=4 << 20),
    )(place, rows, rows_core, *parts)

    height, depth = gradient.shape[1:]
    across = depth // BLK
    chosen = block_ids.reshape(-1)
    flat = jax.ShapeDtypeStruct((height, depth), F32)
    pick = pl.pallas_call(
        pick_kernel,
        in_specs=[VMEM] * 4,
        out_specs=(VMEM,) * 3,
        out_shape=(flat, flat, jax.ShapeDtypeStruct((height, depth), BF16)),
        name="pick",
        compiler_params=pltpu.CompilerParams(vmem_limit_bytes=8 << 20),
    )
    remaining, total, moved = pick(
        (chosen // across).reshape(1, -1), (chosen % across).reshape(1, -1), gradient[0], feedback[0]
    )
    for by in range(1, replicas):
        perm = [(i, (i + by) % replicas) for i in range(replicas)]
        total = total + lax.ppermute(moved, "rep", perm).astype(F32)
    update = total / replicas
    return (output, update, remaining[None])


def solution(mesh):
    in_specs = (
        P(("rep", "exp"), "tp"),
        P(("rep", "exp"), "tp"),
        P(("tp", "exp"), None),
        P(),
        P(("rep", "exp"), None),
        P(("rep", "exp"), None),
        P("exp", None, "tp"),
        P("exp", None, "tp"),
        P("exp", "tp", None),
        P("rep", ("tp", "exp"), None),
        P("rep", ("tp", "exp"), None),
        P("rep", ("tp", "exp"), None),
    )
    out_specs = (P(("rep", "exp"), "tp"), P(("tp", "exp"), None), P("rep", ("tp", "exp"), None))
    return jax.shard_map(layer, mesh=mesh, in_specs=in_specs, out_specs=out_specs, check_vma=False)
```
